32 devices in a mesh: scene: 2 (over x), track: 16 (over z, y, core).
Axes of the slice: x: 2, y: 2, z: 4, core: 2. Of those that a mesh axis runs over, the one named last changes fastest.
Arguments:
- panels: bfloat16 [32, 16, 2, 16, 2048], P(('scene', 'track')), parts along dimension 0, may hold values from -6 to 6
- kernel: bfloat16 [3, 2, 2048, 512], replicated, may hold values from -0.09375 to 0.09375
- steering: float32 [2, 64, 16], replicated, may hold values from -1 to 1
- beam_strips: int32 [32, 3], P('scene'), parts along dimension 0, may hold values from -1 to 15, as said below
- range_blocks: int32 [32, 8], P('scene'), parts along dimension 0, may hold values from 0 to 15
Outputs:
- volume: float32 [2, 64, 16, 4096], P(None, None, 'scene', 'track'), parts along dimension 2
The draws below stay inside these ranges and needn't reach their ends.
There are 2 independent parts, one for each index of `scene`. The reference program is written for one: setup_inputs(seed, part) draws one part's arguments, and reference() takes and returns one part's arrays. A program takes and returns all parts, laid end to end along the dimension named above; an argument that names none is the same for every part. Nothing has to cross between parts.
Inputs may be any that keep to these rules, and one draw needn't show every extreme that they name: `beam_strips`: row b lists the strips c - 1, c, c + 1 for a centre c = b + o with o in -1, 0, 1, each outside 0 .. 15 replaced by -1; block 0 has o <= 0.
All inputs are finite; a program needn't handle non-finite values.
Results may differ from the reference program's by a relative error of at most 0.003.
Values may be sent and summed in bfloat16 or wider, within the bound.
No kernel may reach another device: no remote copies, remote signals or barrier semaphores. Data moves between devices by JAX's collectives and lax.ppermute only.
A program may use at most 64 MiB of HBM per device.

```python
import jax
import jax.numpy as jnp
from jax import lax

TR = 16
RBW = 512
PB = 4
NT = 8
VT = 256
MARGIN = 128
HEIGHTS = 64
BEAMS = 3
NRB = 16
W = 512
BLOCKS = 16


def draw_beam_strips(key, part):
    shift_draw = jax.random.randint(key, (BLOCKS,), -1, 2).astype(jnp.int32)
    position = jnp.arange(BLOCKS, dtype=jnp.int32)
    shift_draw = jnp.where(position == 0, jnp.minimum(shift_draw, 0), shift_draw)
    centre = position + shift_draw
    strips = centre[:, None] + jnp.arange(BEAMS, dtype=jnp.int32)[None, :] - BEAMS // 2
    return jnp.where((strips >= 0) & (strips < BLOCKS), strips, -1).astype(jnp.int32)


def with_ends(array, own_key, least, top_value):
    spot = [jax.random.randint(jax.random.fold_in(own_key, axis), (), 0, length) for axis, length in enumerate(array.shape)]
    main_axis = array.shape.index(max(array.shape))
    next_to = spot[:main_axis] + [(spot[main_axis] + 1) % array.shape[main_axis]] + spot[main_axis + 1:]
    return array.at[tuple(spot)].set(least).at[tuple(next_to)].set(top_value)


def level_of(rng, extent, split, low, high):
    level, own = 1.0, jax.random.fold_in(rng, 6)
    for axis_at, parts in split:
        draws = jnp.exp(jax.random.uniform(jax.random.fold_in(own, axis_at), (parts,), jnp.float32, low / len(split), high / len(split)))
        level = level * jnp.repeat(draws, extent[axis_at] // parts).reshape([-1 if axis == axis_at else 1 for axis in range(len(extent))])
    return level


def gaussian(own_key, dims, spread, bound, cuts=(), held_as=jnp.bfloat16):
    values = jax.random.normal(own_key, dims, jnp.float32) * spread
    if len(cuts) > 0:
        values = level_of(own_key, dims, cuts, -0.22, 0.18) * values
    return jnp.clip(values, min=-bound, max=bound).astype(held_as)


def setup_inputs(seed: int = 0, part: int = 0) -> dict:
    arg_keys = jax.random.split(jax.random.key(seed), 6)
    part_splits = jax.random.split(jax.random.fold_in(arg_keys[5], part), 6)
    panels = gaussian(part_splits[0], (BLOCKS, NRB, 2, TR, PB * RBW), 1.0, 6.0, ((0, 16),))
    kernel = gaussian(arg_keys[1], (BEAMS, 2, PB * RBW, W), (2 * PB * RBW) ** -0.5, 0.09375)
    steering = gaussian(arg_keys[2], (2, HEIGHTS, TR), (2 * TR) ** -0.5, 1.0, (), jnp.float32)
    beam_strips = draw_beam_strips(jax.random.fold_in(jax.random.fold_in(arg_keys[5], part), 71), part)
    range_blocks = with_ends(jax.random.randint(part_splits[4], (BLOCKS, NT), 0, NRB), jax.random.fold_in(part_splits[4], 1), 0, NRB - 1).astype(jnp.int32)
    return {"panels": panels, "kernel": kernel, "steering": steering, "beam_strips": beam_strips, "range_blocks": range_blocks}


def project(panel_shard, kernel_block, tile_rows):
    range_count = panel_shard.shape[0]
    track_count = panel_shard.shape[2]
    span = panel_shard.shape[3]
    panel_rows = panel_shard.reshape(range_count * 2 * track_count, span)
    real_cols = jnp.dot(panel_rows, kernel_block[0], preferred_element_type=jnp.float32)
    imag_cols = jnp.dot(panel_rows, kernel_block[1], preferred_element_type=jnp.float32)
    real_cols = real_cols.reshape(range_count, 2, track_count, -1)
    imag_cols = imag_cols.reshape(range_count, 2, track_count, -1)
    real_part = real_cols[:, 0] - imag_cols[:, 1]
    imag_part = imag_cols[:, 0] + real_cols[:, 1]
    stacked = jnp.stack([real_part, imag_part])
    return jnp.take(stacked, tile_rows, axis=1).astype(jnp.bfloat16)


def reference(panels, kernel, steering, beam_strips, range_blocks):
    strips = beam_strips.shape[0]
    tile_count = range_blocks.shape[1]
    initial = jnp.zeros((2, tile_count, TR, strips, W), jnp.float32)

    def add_block(summed, inputs):
        panel_shard, beam_row = inputs
        for beam_pos in range(BEAMS):
            target = beam_row[beam_pos]
            clipped = jnp.clip(target, 0, strips - 1).astype(jnp.int32)
            contrib = project(panel_shard, kernel[beam_pos], range_blocks[clipped]).astype(jnp.float32)
            contrib = jnp.where(target >= 0, contrib, jnp.zeros_like(contrib))
            summed = summed.at[:, :, :, clipped, :].add(contrib)
        return summed, None

    summed, _ = lax.scan(add_block, initial, (panels, beam_strips))
    centre = summed[..., MARGIN:MARGIN + VT]
    right_tail = summed[..., MARGIN + VT:]
    left_head = summed[..., :MARGIN]
    blank = jnp.zeros_like(right_tail[..., :1, :])
    from_left = jnp.concatenate([blank, right_tail[..., :-1, :]], axis=3)
    from_right = jnp.concatenate([left_head[..., 1:, :], blank], axis=3)
    strip_image = centre + jnp.pad(from_left, ((0, 0), (0, 0), (0, 0), (0, 0), (0, VT - MARGIN)))
    strip_image = strip_image + jnp.pad(from_right, ((0, 0), (0, 0), (0, 0), (0, 0), (VT - MARGIN, 0)))
    strip_image = strip_image.reshape(2, tile_count, TR, strips * VT)
    high = lax.Precision.HIGHEST
    real_vol = jnp.einsum("ht,ntx->hnx", steering[0], strip_image[0], precision=high) - jnp.einsum("ht,ntx->hnx", steering[1], strip_image[1], precision=high)
    imag_vol = jnp.einsum("ht,ntx->hnx", steering[0], strip_image[1], precision=high) + jnp.einsum("ht,ntx->hnx", steering[1], strip_image[0], precision=high)
    return jnp.stack([real_vol, imag_vol])
```

```python
import functools

import jax
import jax.numpy as jnp
from jax import lax
from jax.experimental import pallas as pl
from jax.experimental.pallas import tpu as pltpu
from jax.sharding import PartitionSpec as P

F32 = jnp.float32
BF16 = jnp.bfloat16
VMEM_SPEC = pl.BlockSpec(memory_space=pltpu.VMEM)
SMEM_SPEC = pl.BlockSpec(memory_space=pltpu.SMEM)
ANY_SPEC = pl.BlockSpec(memory_space=pl.ANY)


def backproject(
    strips_ref, ranges_ref, panel_hbm, kernel_hbm,
    swap_ref, far_ref, down_ref, own_ref, up_ref,
    rows, taps, slots, row_sem, tap_sem,
):
    block = lax.axis_index("track")
    beams, _, span, footprint = kernel_hbm.shape
    tiles = ranges_ref.shape[0]
    tracks = panel_hbm.shape[3]
    half = footprint // 4
    cols = footprint // 2
    tile_rows = 2 * tracks

    strip = [strips_ref[j, block] for j in range(beams)]
    row_copies, tap_copies = [], []
    for j in range(beams):
        safe = jnp.maximum(strip[j], 0)
        for t in range(tiles):
            copy = pltpu.make_async_copy(
                panel_hbm.at[0, ranges_ref[t, safe]], rows.at[j, t], row_sem.at[j, t]
            )
            copy.start()
            row_copies.append(copy)
        for part in range(2):
            copy = pltpu.make_async_copy(kernel_hbm.at[j, part], taps.at[j, part], tap_sem.at[j, part])
            copy.start()
            tap_copies.append(copy)

    shift = jnp.int32(0)
    for j in range(beams):
        shift = jnp.where(strip[j] >= 0, strip[j] + 1 - j - block, shift)
    base = 2 * shift + 3
    slots[...] = jnp.zeros_like(slots)

    for j in range(beams):
        lit = strip[j] >= 0
        for t in range(tiles):
            row_copies[j * tiles + t].wait()
        for part in range(2):
            tap_copies[j * 2 + part].wait()
        lhs = rows[j].reshape(tiles * tile_rows, span)
        for c in range(2):
            at = slice(c * cols, (c + 1) * cols)
            q0 = jnp.dot(lhs, taps[j, 0, :, at], preferred_element_type=F32).reshape(tiles, 2, tracks, cols)
            q1 = jnp.dot(lhs, taps[j, 1, :, at], preferred_element_type=F32).reshape(tiles, 2, tracks, cols)
            real = q0[:, 0] - q1[:, 1]
            imag = q1[:, 0] + q0[:, 1]
            both = jnp.concatenate([real, imag], axis=0).reshape(2 * tiles * tracks, cols)
            both = both.astype(BF16).astype(F32)
            both = jnp.where(lit, both, 0.0)
            for q in range(2):
                slots[base + 2 * j + 2 * c + q] += both[:, q * half : (q + 1) * half]

    odd = lax.rem(block, 2)
    first = 4 * (1 - odd)
    for k, s in enumerate((0, 1, 4, 5, 8, 9)):
        swap_ref[k] = slots[first + s].astype(BF16)
    far_ref[...] = slots[jnp.where(odd == 1, 12, 1)].astype(BF16)
    for k in range(2):
        down_ref[k] = slots[2 + k]
        own_ref[k] = slots[6 + k]
        up_ref[k] = slots[10 + k]


def spread(steer_ref, high_ref, low_ref, tiles):
    _, tracks, heights = steer_ref.shape
    n, m = heights * tiles, tiles * tracks
    pick_row = lax.broadcasted_iota(jnp.int32, (n, heights), 0) // tiles
    pick_row = (pick_row == lax.broadcasted_iota(jnp.int32, (n, heights), 1)).astype(BF16)
    pick_col = lax.broadcasted_iota(jnp.int32, (tracks, m), 1) % tracks
    pick_col = (pick_col == lax.broadcasted_iota(jnp.int32, (tracks, m), 0)).astype(BF16)
    same = lax.broadcasted_iota(jnp.int32, (n, m), 0) % tiles
    same = same == lax.broadcasted_iota(jnp.int32, (n, m), 1) // tracks

    def grow(x):
        wide = lax.dot_general(pick_row, x, (((1,), (1,)), ((), ())), preferred_element_type=F32).astype(BF16)
        wide = jnp.dot(wide, pick_col, preferred_element_type=F32)
        return jnp.where(same, wide, 0.0)

    for piece, ref in ((0, high_ref), (1, low_ref)):
        grown = []
        for part in range(2):
            whole = steer_ref[part]
            high = whole.astype(BF16)
            grown.append(grow(high if piece == 0 else (whole - high.astype(F32)).astype(BF16)))
        ref[:n, :m] = grown[0].astype(BF16)
        ref[:n, m:] = (-grown[1]).astype(BF16)
        ref[n:, :m] = grown[1].astype(BF16)
        ref[n:, m:] = grown[0].astype(BF16)


def focus(own_ref, swap_ref, below_ref, above_ref, far_ref, high_ref, low_ref, out_ref, x_high, x_low):
    half = own_ref.shape[2]

    @pl.when(pl.program_id(0) == 0)
    def _():
        odd = lax.rem(lax.axis_index("track"), 2)
        for k in range(2):
            total = own_ref[k] + swap_ref[2 + k].astype(F32)
            total += below_ref[k].astype(F32) + above_ref[k].astype(F32)
            total += jnp.where(odd == k, far_ref[...].astype(F32), 0.0)
            high = total.astype(BF16)
            x_high[:, k * half : (k + 1) * half] = high
            x_low[:, k * half : (k + 1) * half] = (total - high.astype(F32)).astype(BF16)

    a_high, a_low = high_ref[...], low_ref[...]
    out = jnp.dot(a_high, x_high[...], preferred_element_type=F32)
    out += jnp.dot(a_low, x_high[...], preferred_element_type=F32)
    out += jnp.dot(a_high, x_low[...], preferred_element_type=F32)
    out_ref[...] = out.reshape(out_ref.shape)


def body(panels, kernel, steering, beam_strips, range_blocks):
    peers = lax.axis_size("track")
    beams, _, span, footprint = kernel.shape
    tiles = range_blocks.shape[1]
    tracks = panels.shape[3]
    heights = steering.shape[1]
    half = footprint // 4
    rows = 2 * tiles * tracks

    def halves(count, dtype):
        return jax.ShapeDtypeStruct((count, rows, half), dtype)

    swap, far, down, own, up = pl.pallas_call(
        backproject,
        out_shape=(
            halves(6, BF16), jax.ShapeDtypeStruct((rows, half), BF16),
            halves(2, F32), halves(2, F32), halves(2, F32),
        ),
        in_specs=[SMEM_SPEC, SMEM_SPEC, ANY_SPEC, ANY_SPEC],
        out_specs=(VMEM_SPEC,) * 5,
        scratch_shapes=[
            pltpu.VMEM((beams, tiles, 2, tracks, span), BF16),
            pltpu.VMEM((beams, 2, span, footprint), BF16),
            pltpu.VMEM((14, rows, half), F32),
            pltpu.SemaphoreType.DMA((beams, tiles)),
            pltpu.SemaphoreType.DMA((beams, 2)),
        ],
        compiler_params=pltpu.CompilerParams(vmem_limit_bytes=48 << 20),
        cost_estimate=pl.CostEstimate(
            flops=2 * 2 * beams * rows * span * footprint, bytes_accessed=16 << 20, transcendentals=0
        ),
    )(beam_strips.T, range_blocks.T, panels, kernel)

    def send(x, pairs):
        return lax.ppermute(x, "track", [(i, k) for i, k in pairs if 0 <= k < peers])

    swapped = send(swap, [(i, i ^ 1) for i in range(peers)])
    far_got = send(far, [(i, i + 3 if i % 2 else i - 3) for i in range(peers)])
    up_sum = (up + swapped[4:6].astype(F32)).astype(BF16)
    down_sum = (down + swapped[0:2].astype(F32)).astype(BF16)
    below = send(up_sum, [(i, i + 2) for i in range(peers)])
    above = send(down_sum, [(i, i - 2) for i in range(peers)])

    big = jax.ShapeDtypeStruct((2 * heights * tiles, rows), BF16)
    high, low = pl.pallas_call(
        functools.partial(spread, tiles=tiles),
        out_shape=(big, big),
        in_specs=[VMEM_SPEC],
        out_specs=(VMEM_SPEC, VMEM_SPEC),
        cost_estimate=pl.CostEstimate(flops=200_000_000, bytes_accessed=1 << 20, transcendentals=0),
    )(steering.transpose(0, 2, 1))

    steps = 4
    part = heights * 2 // steps
    volume = pl.pallas_call(
        focus,
        grid=(steps,),
        out_shape=jax.ShapeDtypeStruct((2 * heights, tiles, 2 * half), F32),
        in_specs=[
            pl.BlockSpec((2, rows, half), lambda i: (0, 0, 0)),
            pl.BlockSpec((6, rows, half), lambda i: (0, 0, 0)),
            pl.BlockSpec((2, rows, half), lambda i: (0, 0, 0)),
            pl.BlockSpec((2, rows, half), lambda i: (0, 0, 0)),
            pl.BlockSpec((rows, half), lambda i: (0, 0)),
            pl.BlockSpec((part * tiles, rows), lambda i: (i, 0)),
            pl.BlockSpec((part * tiles, rows), lambda i: (i, 0)),
        ],
        out_specs=pl.BlockSpec((part, tiles, 2 * half), lambda i: (i, 0, 0)),
        scratch_shapes=[pltpu.VMEM((rows, 2 * half), BF16), pltpu.VMEM((rows, 2 * half), BF16)],
        cost_estimate=pl.CostEstimate(flops=400_000_000, bytes_accessed=2 << 20, transcendentals=0),
    )(own, swapped, below, above, far_got, high, low)
    return volume.reshape(2, heights, tiles, 2 * half)


def solution(mesh):
    placed = (
        P(("scene", "track"), None, None, None, None),
        P(),
        P(),
        P("scene", None),
        P("scene", None),
    )
    return jax.shard_map(
        body, mesh=mesh, in_specs=placed, out_specs=P(None, None, "scene", "track"), check_vma=False
    )
```

```python
import functools

import jax
import jax.numpy as jnp
from jax import lax
from jax.experimental import pallas as pl
from jax.experimental.pallas import tpu as pltpu
from jax.sharding import PartitionSpec as P


F32 = jnp.float32
BF16 = jnp.bfloat16
VMEM_SPEC = pl.BlockSpec(memory_space=pltpu.VMEM)
HBM_SPEC = pl.BlockSpec(memory_space=pltpu.MemorySpace.HBM)


def backproject(
    strips_hbm, ranges_hbm, panel_hbm, kernel_hbm,
    swap_ref, mid_ref, far_ref, near_ref, own_ref, next_ref,
    strips_ref, ranges_ref, rows, taps, slots, table_sem, row_sem, tap_sem,
):
    block = lax.axis_index("track")
    beams, _, span, footprint = kernel_hbm.shape
    tiles = ranges_ref.shape[0]
    tracks = panel_hbm.shape[3]
    half = footprint // 4
    cols = footprint // 2
    tile_rows = 2 * tracks

    tables = [
        pltpu.make_async_copy(strips_hbm, strips_ref, table_sem.at[0]),
        pltpu.make_async_copy(ranges_hbm, ranges_ref, table_sem.at[1]),
    ]
    for copy in tables:
        copy.start()
    tap_copies = []
    for j in range(beams):
        for c in range(2):
            copy = pltpu.make_async_copy(
                kernel_hbm.at[j, :, :, c * cols : (c + 1) * cols], taps.at[j, c], tap_sem.at[j, c]
            )
            tap_copies.append(copy)
    tap_copies[0].start()
    for copy in tables:
        copy.wait()
    strip = [strips_ref[j, block] for j in range(beams)]
    for j in range(beams):
        safe = jnp.maximum(strip[j], 0)
        for t in range(tiles):
            pltpu.make_async_copy(panel_hbm.at[0, ranges_ref[t, safe]], rows.at[j, t], row_sem.at[j]).start()
        for c in range(2):
            if j + c:
                tap_copies[2 * j + c].start()

    shift = jnp.int32(0)
    for j in range(beams):
        shift = jnp.where(strip[j] >= 0, strip[j] + 1 - j - block, shift)
    base = 2 * shift + 3
    slots[...] = jnp.zeros_like(slots)

    for j in range(beams):
        pltpu.make_async_copy(panel_hbm.at[0, 0:tiles], rows.at[j], row_sem.at[j]).wait()
        for c in range(2):
            tap_copies[2 * j + c].wait()

            @pl.when(strip[j] >= 0)
            def _():
                lhs = rows[j].reshape(tiles * tile_rows, span)
                q0 = jnp.dot(lhs, taps[j, c, 0], preferred_element_type=F32).reshape(tiles, 2, tracks, cols)
                q1 = jnp.dot(lhs, taps[j, c, 1], preferred_element_type=F32).reshape(tiles, 2, tracks, cols)
                parts = (q0[:, 0] - q1[:, 1], q1[:, 0] + q0[:, 1])
                many = tiles * tracks
                for k, part in enumerate(parts):
                    part = part.reshape(many, cols).astype(BF16).astype(F32)
                    for q in range(2):
                        slots[base + 2 * j + 2 * c + q, k * many : (k + 1) * many] += part[:, q * half : (q + 1) * half]

    odd = lax.rem(block, 2)
    first = 4 * (1 - odd)
    upward = 8 * (1 - lax.rem(block // 2, 2))
    for k in range(2):
        swap_ref[k] = slots[first + upward + k].astype(BF16)
        swap_ref[2 + k] = slots[first + 8 - upward + k].astype(BF16)
        near_ref[k] = slots[2 + upward + k]
        next_ref[k] = slots[10 - upward + k]
        mid_ref[k] = slots[first + 4 + k].astype(BF16)
        own_ref[k] = slots[6 + k]
    far_ref[...] = slots[jnp.where(odd == 1, 12, 1)].astype(BF16)


def spread(steer_ref, high_ref, low_ref, tiles):
    _, tracks, heights = steer_ref.shape
    n, m = heights * tiles, tiles * tracks
    pick_row = lax.broadcasted_iota(jnp.int32, (n, heights), 0) // tiles
    pick_row = (pick_row == lax.broadcasted_iota(jnp.int32, (n, heights), 1)).astype(BF16)
    pick_col = lax.broadcasted_iota(jnp.int32, (tracks, m), 1) % tracks
    pick_col = (pick_col == lax.broadcasted_iota(jnp.int32, (tracks, m), 0)).astype(BF16)
    same = lax.broadcasted_iota(jnp.int32, (n, m), 0) % tiles
    same = same == lax.broadcasted_iota(jnp.int32, (n, m), 1) // tracks

    def grow(x):
        wide = lax.dot_general(pick_row, x, (((1,), (1,)), ((), ())), preferred_element_type=F32).astype(BF16)
        wide = jnp.dot(wide, pick_col, preferred_element_type=F32)
        return jnp.where(same, wide, 0.0)

    for piece, ref in ((0, high_ref), (1, low_ref)):
        grown = []
        for part in range(2):
            whole = steer_ref[part]
            high = whole.astype(BF16)
            grown.append(grow(high if piece == 0 else (whole - high.astype(F32)).astype(BF16)))
        ref[:n, :m] = grown[0].astype(BF16)
        ref[:n, m:] = (-grown[1]).astype(BF16)
        ref[n:, :m] = grown[1].astype(BF16)
        ref[n:, m:] = grown[0].astype(BF16)


def focus(own_ref, mid_ref, near_ref, next_ref, far_ref, high_ref, low_ref, out_hbm, x_high, x_low, out, sem, steps):
    half = own_ref.shape[2]
    odd = lax.rem(lax.axis_index("track"), 2)
    for k in range(2):
        total = own_ref[k] + mid_ref[k].astype(F32)
        total += near_ref[k].astype(F32) + next_ref[k].astype(F32)
        total += jnp.where(odd == k, far_ref[...].astype(F32), 0.0)
        high = total.astype(BF16)
        x_high[:, k * half : (k + 1) * half] = high
        x_low[:, k * half : (k + 1) * half] = (total - high.astype(F32)).astype(BF16)

    lines, tiles, width = out.shape
    part = lines // steps
    copies = []
    for i in range(steps):
        at = slice(i * part * tiles, (i + 1) * part * tiles)
        a_high, a_low = high_ref[at], low_ref[at]
        sums = jnp.dot(a_high, x_high[...], preferred_element_type=F32)
        sums += jnp.dot(a_low, x_high[...], preferred_element_type=F32)
        sums += jnp.dot(a_high, x_low[...], preferred_element_type=F32)
        here = pl.ds(i * part, part)
        out[here] = sums.reshape(part, tiles, width)
        copy = pltpu.make_async_copy(out.at[here], out_hbm.at[here], sem.at[i])
        copy.start()
        copies.append(copy)
    for copy in copies:
        copy.wait()


def placed_in(x, name):
    return pltpu.with_memory_space_constraint(x, pltpu.MemorySpace[name])


def body(panels, kernel, steering, beam_strips, range_blocks):
    peers = lax.axis_size("track")
    blocks = beam_strips.shape[0]
    beams, _, span, footprint = kernel.shape
    tiles = range_blocks.shape[1]
    tracks = panels.shape[3]
    heights = steering.shape[1]
    half = footprint // 4
    rows = 2 * tiles * tracks

    def halves(count, dtype):
        return jax.ShapeDtypeStruct((count, rows, half), dtype)

    def send(x, to):
        return lax.ppermute(x, "track", [(i, to(i)) for i in range(peers) if 0 <= to(i) < peers])

    swap, mid, far, near, own, nxt = pl.pallas_call(
        backproject,
        out_shape=(
            halves(4, BF16), halves(2, BF16), jax.ShapeDtypeStruct((rows, half), BF16),
            halves(2, F32), halves(2, F32), halves(2, F32),
        ),
        in_specs=[HBM_SPEC] * 4,
        out_specs=(VMEM_SPEC,) * 6,
        scratch_shapes=[
            pltpu.SMEM((beams, blocks), jnp.int32),
            pltpu.SMEM((tiles, blocks), jnp.int32),
            pltpu.VMEM((beams, tiles, 2, tracks, span), BF16),
            pltpu.VMEM((beams, 2, 2, span, footprint // 2), BF16),
            pltpu.VMEM((14, rows, half), F32),
            pltpu.SemaphoreType.DMA((2,)),
            pltpu.SemaphoreType.DMA((beams,)),
            pltpu.SemaphoreType.DMA((beams, 2)),
        ],
        compiler_params=pltpu.CompilerParams(vmem_limit_bytes=48 << 20),
        cost_estimate=pl.CostEstimate(
            flops=2 * 2 * beams * rows * span * footprint, bytes_accessed=16 << 20, transcendentals=0
        ),
    )(*(placed_in(x, "HBM") for x in (beam_strips.T, range_blocks.T, panels, kernel)))

    swapped = send(swap, lambda i: i ^ 1)
    far_got = send(far, lambda i: i + 3 if i % 2 else i - 3)
    next_sum = (nxt + swapped[2:4].astype(F32)).astype(BF16)
    near_sum = (near + swapped[0:2].astype(F32)).astype(BF16)
    next_got = send(next_sum, lambda i: i + 2 if i // 2 % 2 else i - 2)
    near_got = send(near_sum, lambda i: i - 2 if i // 2 % 2 else i + 2)
    mid_got = send(mid, lambda i: i ^ 1)

    big = jax.ShapeDtypeStruct((2 * heights * tiles, rows), BF16)
    high, low = pl.pallas_call(
        functools.partial(spread, tiles=tiles),
        out_shape=(big, big),
        in_specs=[VMEM_SPEC],
        out_specs=(VMEM_SPEC, VMEM_SPEC),
        compiler_params=pltpu.CompilerParams(vmem_limit_bytes=12 << 20),
        cost_estimate=pl.CostEstimate(flops=200_000_000, bytes_accessed=1 << 20, transcendentals=0),
    )(steering.transpose(0, 2, 1))

    steps = 4
    shape = (2 * heights, tiles, 2 * half)
    volume = pl.pallas_call(
        functools.partial(focus, steps=steps),
        out_shape=jax.ShapeDtypeStruct(shape, F32),
        in_specs=[VMEM_SPEC] * 7,
        out_specs=HBM_SPEC,
        scratch_shapes=[
            pltpu.VMEM((rows, 2 * half), BF16),
            pltpu.VMEM((rows, 2 * half), BF16),
            pltpu.VMEM(shape, F32),
            pltpu.SemaphoreType.DMA((steps,)),
        ],
        compiler_params=pltpu.CompilerParams(vmem_limit_bytes=12 << 20),
        cost_estimate=pl.CostEstimate(flops=400_000_000, bytes_accessed=2 << 20, transcendentals=0),
    )(*(placed_in(x, "VMEM") for x in (own, mid_got, near_got, next_got, far_got, high, low)))
    return volume.reshape(2, heights, tiles, 2 * half)


def solution(mesh):
    placed = (
        P(("scene", "track"), None, None, None, None),
        P(),
        P(),
        P("scene", None),
        P("scene", None),
    )
    return jax.shard_map(
        body, mesh=mesh, in_specs=placed, out_specs=P(None, None, "scene", "track"), check_vma=False
    )
```

```python
import functools

import jax
import jax.numpy as jnp
from jax import lax
from jax.experimental import pallas as pl
from jax.experimental.pallas import tpu as pltpu
from jax.sharding import PartitionSpec as P


F32 = jnp.float32
BF16 = jnp.bfloat16
VMEM_SPEC = pl.BlockSpec(memory_space=pltpu.VMEM)
HBM_SPEC = pl.BlockSpec(memory_space=pltpu.MemorySpace.HBM)


def backproject(
    strips_hbm, ranges_hbm, panel_hbm, kernel_hbm,
    swap_ref, mid_ref, far_ref, near_ref, own_ref, next_ref, own_rows, centre,
    strips_ref, ranges_ref, rows, edges, middles, slots, table_sem, row_sem, tap_sem,
):
    block = lax.axis_index("track")
    beams, _, span, footprint = kernel_hbm.shape
    tiles = ranges_ref.shape[0]
    tracks = panel_hbm.shape[3]
    half = footprint // 4
    cols = footprint // 2
    many = tiles * tracks
    inner = slice(half, half + cols)

    tables = [
        pltpu.make_async_copy(strips_hbm, strips_ref, table_sem.at[0]),
        pltpu.make_async_copy(ranges_hbm, ranges_ref, table_sem.at[1]),
    ]
    for copy in tables:
        copy.start()

    def fetch_edges(j):
        for k, q in enumerate((0, 3)):
            pltpu.make_async_copy(
                kernel_hbm.at[j, :, :, q * half : (q + 1) * half],
                edges.at[j, :, :, k * half : (k + 1) * half],
                tap_sem.at[j],
            ).start()

    order = [beams // 2] + [j for j in range(beams) if j != beams // 2]
    fetch_edges(order[0])
    for copy in tables:
        copy.wait()
    strip = [strips_ref[j, block] for j in range(beams)]
    shift = jnp.int32(0)
    for j in range(beams):
        shift = jnp.where(strip[j] >= 0, strip[j] + 1 - j - block, shift)
    base = 2 * shift + 3
    mine = 1 - shift
    for j in order:
        safe = jnp.maximum(strip[j], 0)
        for t in range(tiles):
            pltpu.make_async_copy(panel_hbm.at[0, ranges_ref[t, safe]], rows.at[j, t], row_sem.at[j]).start()
        if j != order[0]:
            fetch_edges(j)
    for j in order:

        @pl.when(j != mine)
        def _():
            pltpu.make_async_copy(kernel_hbm.at[j, :, :, inner], middles.at[j], tap_sem.at[beams + j]).start()

    for t in range(tiles):
        pltpu.make_async_copy(panel_hbm.at[0, ranges_ref[t, block]], own_rows.at[t], row_sem.at[beams]).start()
    last = pltpu.make_async_copy(kernel_hbm.at[mine, :, :, inner], centre, tap_sem.at[2 * beams])
    last.start()
    slots[...] = jnp.zeros_like(slots)

    def add(lhs, taps, targets):
        q0 = jnp.dot(lhs, taps[0], preferred_element_type=F32).reshape(tiles, 2, tracks, cols)
        q1 = jnp.dot(lhs, taps[1], preferred_element_type=F32).reshape(tiles, 2, tracks, cols)
        parts = (q0[:, 0] - q1[:, 1], q1[:, 0] + q0[:, 1])
        for k, part in enumerate(parts):
            part = part.reshape(many, cols).astype(BF16).astype(F32)
            for n, target in enumerate(targets):
                slots[target, k * many : (k + 1) * many] += part[:, n * half : (n + 1) * half]

    for j in order:
        pltpu.make_async_copy(panel_hbm.at[0, 0:tiles], rows.at[j], row_sem.at[j]).wait()
        pltpu.make_async_copy(kernel_hbm.at[j, :, :, inner], edges.at[j], tap_sem.at[j]).wait()

        @pl.when(strip[j] >= 0)
        def _():
            lhs = rows[j].reshape(2 * many, span)
            add(lhs, edges.at[j], (base + 2 * j, base + 2 * j + 3))

    for j in order:
        whole = pltpu.make_async_copy(kernel_hbm.at[j, :, :, inner], middles.at[j], tap_sem.at[beams + j])

        @pl.when(j != mine)
        def _():
            whole.wait()

        @pl.when((j != mine) & (strip[j] >= 0))
        def _():
            lhs = rows[j].reshape(2 * many, span)
            add(lhs, middles.at[j], (base + 2 * j + 1, base + 2 * j + 2))

    odd = lax.rem(block, 2)
    first = 4 * (1 - odd)
    upward = 8 * (1 - lax.rem(block // 2, 2))
    for k in range(2):
        swap_ref[k] = slots[first + upward + k].astype(BF16)
        swap_ref[2 + k] = slots[first + 8 - upward + k].astype(BF16)
        near_ref[k] = slots[2 + upward + k]
        next_ref[k] = slots[10 - upward + k]
        mid_ref[k] = slots[first + 4 + k].astype(BF16)
        own_ref[k] = slots[6 + k]
    far_ref[...] = slots[jnp.where(odd == 1, 12, 1)].astype(BF16)
    pltpu.make_async_copy(panel_hbm.at[0, 0:tiles], own_rows, row_sem.at[beams]).wait()
    last.wait()


def finish_own(rows, centre, own_ref, out_ref):
    tiles, _, tracks, span = rows.shape
    cols = centre.shape[2]
    half = cols // 2
    many = tiles * tracks
    lhs = rows[...].reshape(2 * many, span)
    q0 = jnp.dot(lhs, centre[0], preferred_element_type=F32).reshape(tiles, 2, tracks, cols)
    q1 = jnp.dot(lhs, centre[1], preferred_element_type=F32).reshape(tiles, 2, tracks, cols)
    parts = (q0[:, 0] - q1[:, 1], q1[:, 0] + q0[:, 1])
    for k, part in enumerate(parts):
        part = part.reshape(many, cols).astype(BF16).astype(F32)
        at = slice(k * many, (k + 1) * many)
        for n in range(2):
            out_ref[n, at] = own_ref[n, at] + part[:, n * half : (n + 1) * half]


def spread(steer_ref, high_ref, low_ref, tiles):
    _, tracks, heights = steer_ref.shape
    n, m = heights * tiles, tiles * tracks
    pick_row = lax.broadcasted_iota(jnp.int32, (n, heights), 0) // tiles
    pick_row = (pick_row == lax.broadcasted_iota(jnp.int32, (n, heights), 1)).astype(BF16)
    pick_col = lax.broadcasted_iota(jnp.int32, (tracks, m), 1) % tracks
    pick_col = (pick_col == lax.broadcasted_iota(jnp.int32, (tracks, m), 0)).astype(BF16)
    same = lax.broadcasted_iota(jnp.int32, (n, m), 0) % tiles
    same = same == lax.broadcasted_iota(jnp.int32, (n, m), 1) // tracks

    def grow(x):
        wide = lax.dot_general(pick_row, x, (((1,), (1,)), ((), ())), preferred_element_type=F32).astype(BF16)
        wide = jnp.dot(wide, pick_col, preferred_element_type=F32)
        return jnp.where(same, wide, 0.0)

    for piece, ref in ((0, high_ref), (1, low_ref)):
        grown = []
        for part in range(2):
            whole = steer_ref[part]
            high = whole.astype(BF16)
            grown.append(grow(high if piece == 0 else (whole - high.astype(F32)).astype(BF16)))
        ref[:n, :m] = grown[0].astype(BF16)
        ref[:n, m:] = (-grown[1]).astype(BF16)
        ref[n:, :m] = grown[1].astype(BF16)
        ref[n:, m:] = grown[0].astype(BF16)


def focus(own_ref, mid_ref, near_ref, next_ref, far_ref, high_ref, low_ref, out_hbm, x_high, x_low, out, sem, steps):
    half = own_ref.shape[2]
    odd = lax.rem(lax.axis_index("track"), 2)
    for k in range(2):
        total = own_ref[k] + mid_ref[k].astype(F32)
        total += near_ref[k].astype(F32) + next_ref[k].astype(F32)
        total += jnp.where(odd == k, far_ref[...].astype(F32), 0.0)
        high = total.astype(BF16)
        x_high[:, k * half : (k + 1) * half] = high
        x_low[:, k * half : (k + 1) * half] = (total - high.astype(F32)).astype(BF16)

    lines, tiles, width = out.shape
    part = lines // steps
    copies = []
    for i in range(steps):
        at = slice(i * part * tiles, (i + 1) * part * tiles)
        a_high, a_low = high_ref[at], low_ref[at]
        sums = jnp.dot(a_high, x_high[...], preferred_element_type=F32)
        sums += jnp.dot(a_low, x_high[...], preferred_element_type=F32)
        sums += jnp.dot(a_high, x_low[...], preferred_element_type=F32)
        here = pl.ds(i * part, part)
        out[here] = sums.reshape(part, tiles, width)
        copy = pltpu.make_async_copy(out.at[here], out_hbm.at[here], sem.at[i])
        copy.start()
        copies.append(copy)
    for copy in copies:
        copy.wait()


def placed_in(x, name):
    return pltpu.with_memory_space_constraint(x, pltpu.MemorySpace[name])


def body(panels, kernel, steering, beam_strips, range_blocks):
    peers = lax.axis_size("track")
    blocks = beam_strips.shape[0]
    beams, _, span, footprint = kernel.shape
    tiles = range_blocks.shape[1]
    tracks = panels.shape[3]
    heights = steering.shape[1]
    half = footprint // 4
    rows = 2 * tiles * tracks

    def halves(count, dtype):
        return jax.ShapeDtypeStruct((count, rows, half), dtype)

    def send(x, to):
        return lax.ppermute(x, "track", [(i, to(i)) for i in range(peers) if 0 <= to(i) < peers])

    swap, mid, far, near, own, nxt, picked, centre = pl.pallas_call(
        backproject,
        out_shape=(
            halves(4, BF16), halves(2, BF16), jax.ShapeDtypeStruct((rows, half), BF16),
            halves(2, F32), halves(2, F32), halves(2, F32),
            jax.ShapeDtypeStruct((tiles, 2, tracks, span), BF16),
            jax.ShapeDtypeStruct((2, span, footprint // 2), BF16),
        ),
        in_specs=[HBM_SPEC] * 4,
        out_specs=(VMEM_SPEC,) * 8,
        scratch_shapes=[
            pltpu.SMEM((beams, blocks), jnp.int32),
            pltpu.SMEM((tiles, blocks), jnp.int32),
            pltpu.VMEM((beams, tiles, 2, tracks, span), BF16),
            pltpu.VMEM((beams, 2, span, footprint // 2), BF16),
            pltpu.VMEM((beams, 2, span, footprint // 2), BF16),
            pltpu.VMEM((14, rows, half), F32),
            pltpu.SemaphoreType.DMA((2,)),
            pltpu.SemaphoreType.DMA((beams + 1,)),
            pltpu.SemaphoreType.DMA((2 * beams + 1,)),
        ],
        compiler_params=pltpu.CompilerParams(vmem_limit_bytes=24 << 20),
        cost_estimate=pl.CostEstimate(
            flops=2 * 2 * beams * rows * span * footprint, bytes_accessed=16 << 20, transcendentals=0
        ),
    )(*(placed_in(x, "HBM") for x in (beam_strips.T, range_blocks.T, panels, kernel)))

    swapped = send(swap, lambda i: i ^ 1)
    far_got = send(far, lambda i: i + 3 if i % 2 else i - 3)
    next_sum = (nxt + swapped[2:4].astype(F32)).astype(BF16)
    near_sum = (near + swapped[0:2].astype(F32)).astype(BF16)
    next_got = send(next_sum, lambda i: i + 2 if i // 2 % 2 else i - 2)
    near_got = send(near_sum, lambda i: i - 2 if i // 2 % 2 else i + 2)
    mid_got = send(mid, lambda i: i ^ 1)

    big = jax.ShapeDtypeStruct((2 * heights * tiles, rows), BF16)
    high, low = pl.pallas_call(
        functools.partial(spread, tiles=tiles),
        out_shape=(big, big),
        in_specs=[VMEM_SPEC],
        out_specs=(VMEM_SPEC, VMEM_SPEC),
        compiler_params=pltpu.CompilerParams(vmem_limit_bytes=12 << 20),
        cost_estimate=pl.CostEstimate(flops=200_000_000, bytes_accessed=1 << 20, transcendentals=0),
    )(steering.transpose(0, 2, 1))

    own = pl.pallas_call(
        finish_own,
        out_shape=halves(2, F32),
        in_specs=[VMEM_SPEC] * 3,
        out_specs=VMEM_SPEC,
        compiler_params=pltpu.CompilerParams(vmem_limit_bytes=12 << 20),
        cost_estimate=pl.CostEstimate(flops=2 * rows * span * footprint, bytes_accessed=1 << 20, transcendentals=0),
    )(*(placed_in(x, "VMEM") for x in (picked, centre, own)))

    steps = 4
    shape = (2 * heights, tiles, 2 * half)
    volume = pl.pallas_call(
        functools.partial(focus, steps=steps),
        out_shape=jax.ShapeDtypeStruct(shape, F32),
        in_specs=[VMEM_SPEC] * 7,
        out_specs=HBM_SPEC,
        scratch_shapes=[
            pltpu.VMEM((rows, 2 * half), BF16),
            pltpu.VMEM((rows, 2 * half), BF16),
            pltpu.VMEM(shape, F32),
            pltpu.SemaphoreType.DMA((steps,)),
        ],
        compiler_params=pltpu.CompilerParams(vmem_limit_bytes=12 << 20),
        cost_estimate=pl.CostEstimate(flops=400_000_000, bytes_accessed=2 << 20, transcendentals=0),
    )(*(placed_in(x, "VMEM") for x in (own, mid_got, near_got, next_got, far_got, high, low)))
    return volume.reshape(2, heights, tiles, 2 * half)


def solution(mesh):
    placed = (
        P(("scene", "track"), None, None, None, None),
        P(),
        P(),
        P("scene", None),
        P("scene", None),
    )
    return jax.shard_map(
        body, mesh=mesh, in_specs=placed, out_specs=P(None, None, "scene", "track"), check_vma=False
    )
```

```python
import functools

import jax
import jax.numpy as jnp
from jax import lax
from jax.experimental import pallas as pl
from jax.experimental.pallas import tpu as pltpu
from jax.sharding import PartitionSpec as P


F32 = jnp.float32
BF16 = jnp.bfloat16
VMEM_SPEC = pl.BlockSpec(memory_space=pltpu.VMEM)
HBM_SPEC = pl.BlockSpec(memory_space=pltpu.MemorySpace.HBM)


def backproject(
    strips_hbm, ranges_hbm, panel_hbm, kernel_hbm,
    swap_ref, cross_ref, mid_ref, far_ref, near_ref, own_ref, next_ref, own_rows, centre,
    strips_ref, ranges_ref, rows, edges, middles, slots, table_sem, row_sem, tap_sem,
):
    block = lax.axis_index("track")
    beams, _, span, footprint = kernel_hbm.shape
    tiles = ranges_ref.shape[0]
    tracks = panel_hbm.shape[3]
    half = footprint // 4
    cols = footprint // 2
    many = tiles * tracks
    inner = slice(half, half + cols)

    tables = [
        pltpu.make_async_copy(strips_hbm, strips_ref, table_sem.at[0]),
        pltpu.make_async_copy(ranges_hbm, ranges_ref, table_sem.at[1]),
    ]
    for copy in tables:
        copy.start()

    def fetch_edges(j):
        for k, q in enumerate((0, 3)):
            pltpu.make_async_copy(
                kernel_hbm.at[j, :, :, q * half : (q + 1) * half],
                edges.at[j, :, :, k * half : (k + 1) * half],
                tap_sem.at[j],
            ).start()

    order = [beams // 2] + [j for j in range(beams) if j != beams // 2]
    fetch_edges(order[0])
    for copy in tables:
        copy.wait()
    strip = [strips_ref[j, block] for j in range(beams)]
    shift = jnp.int32(0)
    for j in range(beams):
        shift = jnp.where(strip[j] >= 0, strip[j] + 1 - j - block, shift)
    base = 2 * shift + 3
    mine = 1 - shift
    for j in order:
        safe = jnp.maximum(strip[j], 0)
        for t in range(tiles):
            pltpu.make_async_copy(panel_hbm.at[0, ranges_ref[t, safe]], rows.at[j, t], row_sem.at[j]).start()
        if j != order[0]:
            fetch_edges(j)
    for j in order:

        @pl.when(j != mine)
        def _():
            pltpu.make_async_copy(kernel_hbm.at[j, :, :, inner], middles.at[j], tap_sem.at[beams + j]).start()

    for t in range(tiles):
        pltpu.make_async_copy(panel_hbm.at[0, ranges_ref[t, block]], own_rows.at[t], row_sem.at[beams]).start()
    last = pltpu.make_async_copy(kernel_hbm.at[mine, :, :, inner], centre, tap_sem.at[2 * beams])
    last.start()
    slots[...] = jnp.zeros_like(slots)

    def add(lhs, taps, targets):
        q0 = jnp.dot(lhs, taps[0], preferred_element_type=F32).reshape(tiles, 2, tracks, cols)
        q1 = jnp.dot(lhs, taps[1], preferred_element_type=F32).reshape(tiles, 2, tracks, cols)
        parts = (q0[:, 0] - q1[:, 1], q1[:, 0] + q0[:, 1])
        for k, part in enumerate(parts):
            part = part.reshape(many, cols).astype(BF16).astype(F32)
            for n, target in enumerate(targets):
                slots[target, k * many : (k + 1) * many] += part[:, n * half : (n + 1) * half]

    for j in order:
        pltpu.make_async_copy(panel_hbm.at[0, 0:tiles], rows.at[j], row_sem.at[j]).wait()
        pltpu.make_async_copy(kernel_hbm.at[j, :, :, inner], edges.at[j], tap_sem.at[j]).wait()

        @pl.when(strip[j] >= 0)
        def _():
            lhs = rows[j].reshape(2 * many, span)
            add(lhs, edges.at[j], (base + 2 * j, base + 2 * j + 3))

    for j in order:
        whole = pltpu.make_async_copy(kernel_hbm.at[j, :, :, inner], middles.at[j], tap_sem.at[beams + j])

        @pl.when(j != mine)
        def _():
            whole.wait()

        @pl.when((j != mine) & (strip[j] >= 0))
        def _():
            lhs = rows[j].reshape(2 * many, span)
            add(lhs, middles.at[j], (base + 2 * j + 1, base + 2 * j + 2))

    odd = lax.rem(block, 2)
    first = 4 * (1 - odd)
    upward = 8 * (1 - lax.rem(block // 2, 2))
    for k in range(2):
        swap_ref[k] = slots[first + upward + k].astype(BF16)
        cross_ref[k] = slots[first + 8 - upward + k].astype(BF16)
        near_ref[k] = slots[2 + upward + k]
        next_ref[k] = slots[10 - upward + k]
        mid_ref[k] = slots[first + 4 + k].astype(BF16)
        own_ref[k] = slots[6 + k]
    far_ref[...] = slots[jnp.where(odd == 1, 12, 1)].astype(BF16)
    pltpu.make_async_copy(panel_hbm.at[0, 0:tiles], own_rows, row_sem.at[beams]).wait()
    last.wait()


def finish_own(rows, centre, own_ref, out_ref):
    tiles, _, tracks, span = rows.shape
    cols = centre.shape[2]
    half = cols // 2
    many = tiles * tracks
    lhs = rows[...].reshape(2 * many, span)
    q0 = jnp.dot(lhs, centre[0], preferred_element_type=F32).reshape(tiles, 2, tracks, cols)
    q1 = jnp.dot(lhs, centre[1], preferred_element_type=F32).reshape(tiles, 2, tracks, cols)
    parts = (q0[:, 0] - q1[:, 1], q1[:, 0] + q0[:, 1])
    for k, part in enumerate(parts):
        part = part.reshape(many, cols).astype(BF16).astype(F32)
        at = slice(k * many, (k + 1) * many)
        for n in range(2):
            out_ref[n, at] = own_ref[n, at] + part[:, n * half : (n + 1) * half]


def fold(steer_ref, out_ref):
    _, tracks, heights = steer_ref.shape
    same = lax.broadcasted_iota(jnp.int32, (heights, heights), 0)
    same = (same == lax.broadcasted_iota(jnp.int32, (heights, heights), 1)).astype(BF16)
    width = out_ref.shape[1]

    def turned(x):
        return lax.dot_general(same, x, (((1,), (1,)), ((), ())), preferred_element_type=F32).astype(BF16)

    def put(x, *starts):
        row = lax.broadcasted_iota(jnp.int32, (tracks, width), 0)
        col = lax.broadcasted_iota(jnp.int32, (tracks, width), 1)
        where = functools.reduce(jnp.logical_or, [col == row + start * tracks for start in starts])
        return jnp.dot(x, where.astype(BF16), preferred_element_type=F32)

    high, low = [], []
    for part in range(2):
        whole = steer_ref[part]
        top = whole.astype(BF16)
        high.append(turned(top))
        low.append(turned((whole - top.astype(F32)).astype(BF16)))
    real = put(high[0], 0, 2) + put(-high[1], 1, 3) + put(low[0], 4) + put(-low[1], 5)
    imag = put(high[1], 0, 2) + put(high[0], 1, 3) + put(low[1], 4) + put(low[0], 5)
    out_ref[:heights] = real.astype(BF16)
    out_ref[heights:] = imag.astype(BF16)


def focus(own_ref, mid_ref, near_ref, next_ref, far_ref, matrix_ref, out_hbm, pieces, out, sem):
    _, lines, tiles, half = out.shape
    tracks = own_ref.shape[1] // (2 * tiles)
    odd = lax.rem(lax.axis_index("track"), 2)
    for k in range(2):
        total = own_ref[k] + mid_ref[k].astype(F32)
        total += near_ref[k].astype(F32) + next_ref[k].astype(F32)
        total += jnp.where(odd == k, far_ref[...].astype(F32), 0.0)
        high = total.astype(BF16)
        low = (total - high.astype(F32)).astype(BF16)
        cols = slice(k * half, (k + 1) * half)
        for part in range(2):
            for tile in range(tiles):
                start = (part * tiles + tile) * tracks
                for place, piece in enumerate((high, low, high)):
                    to = (2 * place + part) * tracks
                    pieces[tile, to : to + tracks, cols] = piece[start : start + tracks]

    steps = sem.shape[0]
    count = lines // steps
    copies = []
    for i in range(steps):
        matrix = matrix_ref[i * count : (i + 1) * count]
        for tile in range(tiles):
            sums = jnp.dot(matrix, pieces[tile], preferred_element_type=F32)
            for k in range(2):
                flat = out.at[k].reshape(lines * tiles, half)
                flat[pl.ds(i * count * tiles + tile, count, stride=tiles)] = sums[:, k * half : (k + 1) * half]
        here = pl.ds(i * count, count)
        for k in range(2):
            copy = pltpu.make_async_copy(
                out.at[k, here], out_hbm.at[here, :, k * half : (k + 1) * half], sem.at[i, k]
            )
            copy.start()
            copies.append(copy)
    for copy in copies:
        copy.wait()


def placed_in(x, name):
    return pltpu.with_memory_space_constraint(x, pltpu.MemorySpace[name])


def body(panels, kernel, steering, beam_strips, range_blocks):
    peers = lax.axis_size("track")
    blocks = beam_strips.shape[0]
    beams, _, span, footprint = kernel.shape
    tiles = range_blocks.shape[1]
    tracks = panels.shape[3]
    heights = steering.shape[1]
    half = footprint // 4
    rows = 2 * tiles * tracks

    def halves(count, dtype):
        return jax.ShapeDtypeStruct((count, rows, half), dtype)

    def send(x, to):
        return lax.ppermute(x, "track", [(i, to(i)) for i in range(peers) if 0 <= to(i) < peers])

    swap, cross, mid, far, near, own, nxt, picked, centre = pl.pallas_call(
        backproject,
        out_shape=(
            halves(2, BF16), halves(2, BF16), halves(2, BF16), jax.ShapeDtypeStruct((rows, half), BF16),
            halves(2, F32), halves(2, F32), halves(2, F32),
            jax.ShapeDtypeStruct((tiles, 2, tracks, span), BF16),
            jax.ShapeDtypeStruct((2, span, footprint // 2), BF16),
        ),
        in_specs=[HBM_SPEC] * 4,
        out_specs=(VMEM_SPEC,) * 9,
        scratch_shapes=[
            pltpu.SMEM((beams, blocks), jnp.int32),
            pltpu.SMEM((tiles, blocks), jnp.int32),
            pltpu.VMEM((beams, tiles, 2, tracks, span), BF16),
            pltpu.VMEM((beams, 2, span, footprint // 2), BF16),
            pltpu.VMEM((beams, 2, span, footprint // 2), BF16),
            pltpu.VMEM((14, rows, half), F32),
            pltpu.SemaphoreType.DMA((2,)),
            pltpu.SemaphoreType.DMA((beams + 1,)),
            pltpu.SemaphoreType.DMA((2 * beams + 1,)),
        ],
        compiler_params=pltpu.CompilerParams(vmem_limit_bytes=24 << 20),
        cost_estimate=pl.CostEstimate(
            flops=2 * 2 * beams * rows * span * footprint, bytes_accessed=16 << 20, transcendentals=0
        ),
    )(*(placed_in(x, "HBM") for x in (beam_strips.T, range_blocks.T, panels, kernel)))

    swapped = send(swap, lambda i: i ^ 1)
    crossed = send(cross, lambda i: i ^ 1)
    far_got = send(far, lambda i: i + 3 if i % 2 else i - 3)
    next_sum = (nxt + crossed.astype(F32)).astype(BF16)
    near_sum = (near + swapped.astype(F32)).astype(BF16)
    next_got = send(next_sum, lambda i: i + 2 if i // 2 % 2 else i - 2)
    near_got = send(near_sum, lambda i: i - 2 if i // 2 % 2 else i + 2)
    mid_got = send(mid, lambda i: i ^ 1)

    matrix = pl.pallas_call(
        fold,
        out_shape=jax.ShapeDtypeStruct((2 * heights, 6 * tracks), BF16),
        in_specs=[VMEM_SPEC],
        out_specs=VMEM_SPEC,
        compiler_params=pltpu.CompilerParams(vmem_limit_bytes=12 << 20),
        cost_estimate=pl.CostEstimate(flops=10_000_000, bytes_accessed=1 << 15, transcendentals=0),
    )(steering.transpose(0, 2, 1))

    own = pl.pallas_call(
        finish_own,
        out_shape=halves(2, F32),
        in_specs=[VMEM_SPEC] * 3,
        out_specs=VMEM_SPEC,
        compiler_params=pltpu.CompilerParams(vmem_limit_bytes=12 << 20),
        cost_estimate=pl.CostEstimate(flops=2 * rows * span * footprint, bytes_accessed=1 << 20, transcendentals=0),
    )(*(placed_in(x, "VMEM") for x in (picked, centre, own)))

    steps = 2
    volume = pl.pallas_call(
        focus,
        out_shape=jax.ShapeDtypeStruct((2 * heights, tiles, 2 * half), F32),
        in_specs=[VMEM_SPEC] * 6,
        out_specs=HBM_SPEC,
        scratch_shapes=[
            pltpu.VMEM((tiles, 6 * tracks, 2 * half), BF16),
            pltpu.VMEM((2, 2 * heights, tiles, half), F32),
            pltpu.SemaphoreType.DMA((steps, 2)),
        ],
        compiler_params=pltpu.CompilerParams(vmem_limit_bytes=12 << 20),
        cost_estimate=pl.CostEstimate(flops=100_000_000, bytes_accessed=2 << 20, transcendentals=0),
    )(*(placed_in(x, "VMEM") for x in (own, mid_got, near_got, next_got, far_got, matrix)))
    return volume.reshape(2, heights, tiles, 2 * half)


def solution(mesh):
    placed = (
        P(("scene", "track"), None, None, None, None),
        P(),
        P(),
        P("scene", None),
        P("scene", None),
    )
    return jax.shard_map(
        body, mesh=mesh, in_specs=placed, out_specs=P(None, None, "scene", "track"), check_vma=False
    )
```

```python
import functools

import jax
import jax.numpy as jnp
from jax import lax
from jax.experimental import pallas as pl
from jax.experimental.pallas import tpu as pltpu
from jax.sharding import PartitionSpec as P


F32 = jnp.float32
BF16 = jnp.bfloat16
VMEM_SPEC = pl.BlockSpec(memory_space=pltpu.VMEM)
HBM_SPEC = pl.BlockSpec(memory_space=pltpu.MemorySpace.HBM)


def backproject(
    strips_hbm, ranges_hbm, panel_hbm, kernel_hbm,
    swap_ref, cross_ref, mid_ref, far_ref, near_ref, own_ref, next_ref, own_rows, centre,
    strips_ref, ranges_ref, rows, edges, middles, slots, table_sem, row_sem, tap_sem,
):
    block = lax.axis_index("track")
    beams, _, span, footprint = kernel_hbm.shape
    tiles = ranges_ref.shape[0]
    tracks = panel_hbm.shape[3]
    half = footprint // 4
    cols = footprint // 2
    many = tiles * tracks
    inner = slice(half, half + cols)

    tables = [
        pltpu.make_async_copy(strips_hbm, strips_ref, table_sem.at[0]),
        pltpu.make_async_copy(ranges_hbm, ranges_ref, table_sem.at[1]),
    ]
    for copy in tables:
        copy.start()

    def fetch_edges(j):
        for k, q in enumerate((0, 3)):
            pltpu.make_async_copy(
                kernel_hbm.at[j, :, :, q * half : (q + 1) * half],
                edges.at[j, :, :, k * half : (k + 1) * half],
                tap_sem.at[j],
            ).start()

    order = [beams // 2] + [j for j in range(beams) if j != beams // 2]
    fetch_edges(order[0])
    for copy in tables:
        copy.wait()
    strip = [strips_ref[j, block] for j in range(beams)]
    shift = jnp.int32(0)
    for j in range(beams):
        shift = jnp.where(strip[j] >= 0, strip[j] + 1 - j - block, shift)
    base = 2 * shift + 3
    mine = 1 - shift
    for j in order:
        safe = jnp.maximum(strip[j], 0)
        for t in range(tiles):
            pltpu.make_async_copy(panel_hbm.at[0, ranges_ref[t, safe]], rows.at[j, t], row_sem.at[j]).start()
        if j != order[0]:
            fetch_edges(j)
    for j in order:

        @pl.when(j != mine)
        def _():
            pltpu.make_async_copy(kernel_hbm.at[j, :, :, inner], middles.at[j], tap_sem.at[beams + j]).start()

    for t in range(tiles):
        pltpu.make_async_copy(panel_hbm.at[0, ranges_ref[t, block]], own_rows.at[t], row_sem.at[beams]).start()
    last = pltpu.make_async_copy(kernel_hbm.at[mine, :, :, inner], centre, tap_sem.at[2 * beams])
    last.start()
    slots[...] = jnp.zeros_like(slots)

    def add(lhs, taps, targets):
        q0 = jnp.dot(lhs, taps[0], preferred_element_type=F32).reshape(tiles, 2, tracks, cols)
        q1 = jnp.dot(lhs, taps[1], preferred_element_type=F32).reshape(tiles, 2, tracks, cols)
        parts = (q0[:, 0] - q1[:, 1], q1[:, 0] + q0[:, 1])
        for k, part in enumerate(parts):
            part = part.reshape(many, cols).astype(BF16).astype(F32)
            for n, target in enumerate(targets):
                slots[target, k * many : (k + 1) * many] += part[:, n * half : (n + 1) * half]

    for j in order:
        pltpu.make_async_copy(panel_hbm.at[0, 0:tiles], rows.at[j], row_sem.at[j]).wait()
        pltpu.make_async_copy(kernel_hbm.at[j, :, :, inner], edges.at[j], tap_sem.at[j]).wait()

        @pl.when(strip[j] >= 0)
        def _():
            lhs = rows[j].reshape(2 * many, span)
            add(lhs, edges.at[j], (base + 2 * j, base + 2 * j + 3))

    for j in order:
        whole = pltpu.make_async_copy(kernel_hbm.at[j, :, :, inner], middles.at[j], tap_sem.at[beams + j])

        @pl.when(j != mine)
        def _():
            whole.wait()

        @pl.when((j != mine) & (strip[j] >= 0))
        def _():
            lhs = rows[j].reshape(2 * many, span)
            add(lhs, middles.at[j], (base + 2 * j + 1, base + 2 * j + 2))

    odd = lax.rem(block, 2)
    first = 4 * (1 - odd)
    upward = 8 * (1 - lax.rem(block // 2, 2))
    for k in range(2):
        swap_ref[k] = slots[2 + upward + k].astype(BF16)
        cross_ref[k] = slots[first + 8 - upward + k].astype(BF16)
        near_ref[k] = slots[first + upward + k]
        next_ref[k] = slots[10 - upward + k]
        mid_ref[k] = slots[first + 4 + k].astype(BF16)
        own_ref[k] = slots[6 + k]
    far_ref[...] = slots[jnp.where(odd == 1, 12, 1)].astype(BF16)
    pltpu.make_async_copy(panel_hbm.at[0, 0:tiles], own_rows, row_sem.at[beams]).wait()
    last.wait()


def finish_own(rows, centre, own_ref, out_ref):
    tiles, _, tracks, span = rows.shape
    cols = centre.shape[2]
    half = cols // 2
    many = tiles * tracks
    lhs = rows[...].reshape(2 * many, span)
    q0 = jnp.dot(lhs, centre[0], preferred_element_type=F32).reshape(tiles, 2, tracks, cols)
    q1 = jnp.dot(lhs, centre[1], preferred_element_type=F32).reshape(tiles, 2, tracks, cols)
    parts = (q0[:, 0] - q1[:, 1], q1[:, 0] + q0[:, 1])
    for k, part in enumerate(parts):
        part = part.reshape(many, cols).astype(BF16).astype(F32)
        at = slice(k * many, (k + 1) * many)
        for n in range(2):
            out_ref[n, at] = own_ref[n, at] + part[:, n * half : (n + 1) * half]


def fold(steer_ref, out_ref):
    _, tracks, heights = steer_ref.shape
    same = lax.broadcasted_iota(jnp.int32, (heights, heights), 0)
    same = (same == lax.broadcasted_iota(jnp.int32, (heights, heights), 1)).astype(BF16)
    width = out_ref.shape[1]

    def turned(x):
        return lax.dot_general(same, x, (((1,), (1,)), ((), ())), preferred_element_type=F32).astype(BF16)

    def put(x, *starts):
        row = lax.broadcasted_iota(jnp.int32, (tracks, width), 0)
        col = lax.broadcasted_iota(jnp.int32, (tracks, width), 1)
        where = functools.reduce(jnp.logical_or, [col == row + start * tracks for start in starts])
        return jnp.dot(x, where.astype(BF16), preferred_element_type=F32)

    high, low = [], []
    for part in range(2):
        whole = steer_ref[part]
        top = whole.astype(BF16)
        high.append(turned(top))
        low.append(turned((whole - top.astype(F32)).astype(BF16)))
    real = put(high[0], 0, 2) + put(-high[1], 1, 3) + put(low[0], 4) + put(-low[1], 5)
    imag = put(high[1], 0, 2) + put(high[0], 1, 3) + put(low[1], 4) + put(low[0], 5)
    out_ref[:heights] = real.astype(BF16)
    out_ref[heights:] = imag.astype(BF16)


def focus(own_ref, mid_ref, near_ref, next_ref, far_ref, matrix_ref, out_hbm, pieces, out, sem):
    _, lines, tiles, half = out.shape
    tracks = own_ref.shape[1] // (2 * tiles)
    odd = lax.rem(lax.axis_index("track"), 2)
    for k in range(2):
        total = own_ref[k] + mid_ref[k].astype(F32)
        total += near_ref[k].astype(F32) + next_ref[k].astype(F32)
        total += jnp.where(odd == k, far_ref[...].astype(F32), 0.0)
        high = total.astype(BF16)
        low = (total - high.astype(F32)).astype(BF16)
        cols = slice(k * half, (k + 1) * half)
        for part in range(2):
            for tile in range(tiles):
                start = (part * tiles + tile) * tracks
                for place, piece in enumerate((high, low, high)):
                    to = (2 * place + part) * tracks
                    pieces[tile, to : to + tracks, cols] = piece[start : start + tracks]

    steps = sem.shape[0]
    count = lines // steps
    copies = []
    for i in range(steps):
        matrix = matrix_ref[i * count : (i + 1) * count]
        for tile in range(tiles):
            sums = jnp.dot(matrix, pieces[tile], preferred_element_type=F32)
            for k in range(2):
                flat = out.at[k].reshape(lines * tiles, half)
                flat[pl.ds(i * count * tiles + tile, count, stride=tiles)] = sums[:, k * half : (k + 1) * half]
        here = pl.ds(i * count, count)
        for k in range(2):
            copy = pltpu.make_async_copy(
                out.at[k, here], out_hbm.at[here, :, k * half : (k + 1) * half], sem.at[i, k]
            )
            copy.start()
            copies.append(copy)
    for copy in copies:
        copy.wait()


def placed_in(x, name):
    return pltpu.with_memory_space_constraint(x, pltpu.MemorySpace[name])


def body(panels, kernel, steering, beam_strips, range_blocks):
    peers = lax.axis_size("track")
    blocks = beam_strips.shape[0]
    beams, _, span, footprint = kernel.shape
    tiles = range_blocks.shape[1]
    tracks = panels.shape[3]
    heights = steering.shape[1]
    half = footprint // 4
    rows = 2 * tiles * tracks

    def halves(count, dtype):
        return jax.ShapeDtypeStruct((count, rows, half), dtype)

    def send(x, to):
        return lax.ppermute(x, "track", [(i, to(i)) for i in range(peers) if 0 <= to(i) < peers])

    swap, cross, mid, far, near, own, nxt, picked, centre = pl.pallas_call(
        backproject,
        out_shape=(
            halves(2, BF16), halves(2, BF16), halves(2, BF16), jax.ShapeDtypeStruct((rows, half), BF16),
            halves(2, F32), halves(2, F32), halves(2, F32),
            jax.ShapeDtypeStruct((tiles, 2, tracks, span), BF16),
            jax.ShapeDtypeStruct((2, span, footprint // 2), BF16),
        ),
        in_specs=[HBM_SPEC] * 4,
        out_specs=(VMEM_SPEC,) * 9,
        scratch_shapes=[
            pltpu.SMEM((beams, blocks), jnp.int32),
            pltpu.SMEM((tiles, blocks), jnp.int32),
            pltpu.VMEM((beams, tiles, 2, tracks, span), BF16),
            pltpu.VMEM((beams, 2, span, footprint // 2), BF16),
            pltpu.VMEM((beams, 2, span, footprint // 2), BF16),
            pltpu.VMEM((14, rows, half), F32),
            pltpu.SemaphoreType.DMA((2,)),
            pltpu.SemaphoreType.DMA((beams + 1,)),
            pltpu.SemaphoreType.DMA((2 * beams + 1,)),
        ],
        compiler_params=pltpu.CompilerParams(vmem_limit_bytes=24 << 20),
        cost_estimate=pl.CostEstimate(
            flops=2 * 2 * beams * rows * span * footprint, bytes_accessed=16 << 20, transcendentals=0
        ),
    )(*(placed_in(x, "HBM") for x in (beam_strips.T, range_blocks.T, panels, kernel)))

    swapped = send(swap, lambda i: i ^ 1)
    crossed = send(cross, lambda i: i ^ 1)
    far_got = send(far, lambda i: i + 3 if i % 2 else i - 3)
    next_sum = (nxt + crossed.astype(F32)).astype(BF16)
    near_sum = (near + swapped.astype(F32)).astype(BF16)
    next_got = send(next_sum, lambda i: i + 2 if i // 2 % 2 else i - 2)
    near_got = send(near_sum, lambda i: i ^ 3)
    mid_got = send(mid, lambda i: i ^ 1)

    matrix = pl.pallas_call(
        fold,
        out_shape=jax.ShapeDtypeStruct((2 * heights, 6 * tracks), BF16),
        in_specs=[VMEM_SPEC],
        out_specs=VMEM_SPEC,
        compiler_params=pltpu.CompilerParams(vmem_limit_bytes=12 << 20),
        cost_estimate=pl.CostEstimate(flops=10_000_000, bytes_accessed=1 << 15, transcendentals=0),
    )(steering.transpose(0, 2, 1))

    own = pl.pallas_call(
        finish_own,
        out_shape=halves(2, F32),
        in_specs=[VMEM_SPEC] * 3,
        out_specs=VMEM_SPEC,
        compiler_params=pltpu.CompilerParams(vmem_limit_bytes=12 << 20),
        cost_estimate=pl.CostEstimate(flops=2 * rows * span * footprint, bytes_accessed=1 << 20, transcendentals=0),
    )(*(placed_in(x, "VMEM") for x in (picked, centre, own)))

    steps = 2
    volume = pl.pallas_call(
        focus,
        out_shape=jax.ShapeDtypeStruct((2 * heights, tiles, 2 * half), F32),
        in_specs=[VMEM_SPEC] * 6,
        out_specs=HBM_SPEC,
        scratch_shapes=[
            pltpu.VMEM((tiles, 6 * tracks, 2 * half), BF16),
            pltpu.VMEM((2, 2 * heights, tiles, half), F32),
            pltpu.SemaphoreType.DMA((steps, 2)),
        ],
        compiler_params=pltpu.CompilerParams(vmem_limit_bytes=12 << 20),
        cost_estimate=pl.CostEstimate(flops=100_000_000, bytes_accessed=2 << 20, transcendentals=0),
    )(*(placed_in(x, "VMEM") for x in (own, mid_got, near_got, next_got, far_got, matrix)))
    return volume.reshape(2, heights, tiles, 2 * half)


def solution(mesh):
    placed = (
        P(("scene", "track"), None, None, None, None),
        P(),
        P(),
        P("scene", None),
        P("scene", None),
    )
    return jax.shard_map(
        body, mesh=mesh, in_specs=placed, out_specs=P(None, None, "scene", "track"), check_vma=False
    )
```

```python
import functools

import jax
import jax.numpy as jnp
from jax import lax
from jax.experimental import pallas as pl
from jax.experimental.pallas import tpu as pltpu
from jax.sharding import PartitionSpec as P


F32 = jnp.float32
BF16 = jnp.bfloat16
VMEM_SPEC = pl.BlockSpec(memory_space=pltpu.VMEM)
HBM_SPEC = pl.BlockSpec(memory_space=pltpu.MemorySpace.HBM)


def backproject(
    strips_hbm, ranges_hbm, panel_hbm, kernel_hbm,
    swap_ref, cross_ref, mid_ref, far_ref, near_ref, own_ref, next_ref, own_rows, centre,
    strips_ref, ranges_ref, rows, edges, middles, slots, table_sem, row_sem, tap_sem,
):
    block = lax.axis_index("track")
    beams, _, span, footprint = kernel_hbm.shape
    tiles = ranges_ref.shape[0]
    tracks = panel_hbm.shape[3]
    half = footprint // 4
    cols = footprint // 2
    many = tiles * tracks
    inner = slice(half, half + cols)

    tables = [
        pltpu.make_async_copy(strips_hbm, strips_ref, table_sem.at[0]),
        pltpu.make_async_copy(ranges_hbm, ranges_ref, table_sem.at[1]),
    ]
    for copy in tables:
        copy.start()

    def fetch_edges(j):
        for k, q in enumerate((0, 3)):
            pltpu.make_async_copy(
                kernel_hbm.at[j, :, :, q * half : (q + 1) * half],
                edges.at[j, :, :, k * half : (k + 1) * half],
                tap_sem.at[j],
            ).start()

    order = [beams // 2] + [j for j in range(beams) if j != beams // 2]
    fetch_edges(order[0])
    for copy in tables:
        copy.wait()
    strip = [strips_ref[j, block] for j in range(beams)]
    shift = jnp.int32(0)
    for j in range(beams):
        shift = jnp.where(strip[j] >= 0, strip[j] + 1 - j - block, shift)
    base = 2 * shift + 3
    mine = 1 - shift
    for j in order:
        safe = jnp.maximum(strip[j], 0)
        for t in range(tiles):
            pltpu.make_async_copy(panel_hbm.at[0, ranges_ref[t, safe]], rows.at[j, t], row_sem.at[j]).start()
        if j != order[0]:
            fetch_edges(j)
    for j in order:

        @pl.when(j != mine)
        def _():
            pltpu.make_async_copy(kernel_hbm.at[j, :, :, inner], middles.at[j], tap_sem.at[beams + j]).start()

    for t in range(tiles):
        pltpu.make_async_copy(panel_hbm.at[0, ranges_ref[t, block]], own_rows.at[t], row_sem.at[beams]).start()
    last = pltpu.make_async_copy(kernel_hbm.at[mine, :, :, inner], centre, tap_sem.at[2 * beams])
    last.start()
    slots[...] = jnp.zeros_like(slots)

    def add(lhs, taps, targets):
        q0 = jnp.dot(lhs, taps[0], preferred_element_type=F32).reshape(tiles, 2, tracks, cols)
        q1 = jnp.dot(lhs, taps[1], preferred_element_type=F32).reshape(tiles, 2, tracks, cols)
        parts = (q0[:, 0] - q1[:, 1], q1[:, 0] + q0[:, 1])
        for k, part in enumerate(parts):
            part = part.reshape(many, cols).astype(BF16).astype(F32)
            for n, target in enumerate(targets):
                slots[target, k * many : (k + 1) * many] += part[:, n * half : (n + 1) * half]

    for j in order:
        pltpu.make_async_copy(panel_hbm.at[0, 0:tiles], rows.at[j], row_sem.at[j]).wait()
        pltpu.make_async_copy(kernel_hbm.at[j, :, :, inner], edges.at[j], tap_sem.at[j]).wait()

        @pl.when(strip[j] >= 0)
        def _():
            lhs = rows[j].reshape(2 * many, span)
            add(lhs, edges.at[j], (base + 2 * j, base + 2 * j + 3))

    for j in order:
        whole = pltpu.make_async_copy(kernel_hbm.at[j, :, :, inner], middles.at[j], tap_sem.at[beams + j])

        @pl.when(j != mine)
        def _():
            whole.wait()

        @pl.when((j != mine) & (strip[j] >= 0))
        def _():
            lhs = rows[j].reshape(2 * many, span)
            add(lhs, middles.at[j], (base + 2 * j + 1, base + 2 * j + 2))

    odd = lax.rem(block, 2)
    first = 4 * (1 - odd)
    upward = 8 * (1 - lax.rem(block // 2, 2))
    for k in range(2):
        swap_ref[k] = slots[2 + upward + k].astype(BF16)
        cross_ref[k] = slots[first + 8 - upward + k].astype(BF16)
        near_ref[k] = slots[first + upward + k]
        next_ref[k] = slots[10 - upward + k]
        mid_ref[k] = slots[first + 4 + k].astype(BF16)
        own_ref[k] = slots[6 + k]
    far_ref[...] = slots[jnp.where(odd == 1, 12, 1)].astype(BF16)
    pltpu.make_async_copy(panel_hbm.at[0, 0:tiles], own_rows, row_sem.at[beams]).wait()
    last.wait()


def finish_own(rows, centre, own_ref, near_ref, out_ref):
    tiles, _, tracks, span = rows.shape
    cols = centre.shape[2]
    half = cols // 2
    many = tiles * tracks
    lhs = rows[...].reshape(2 * many, span)
    q0 = jnp.dot(lhs, centre[0], preferred_element_type=F32).reshape(tiles, 2, tracks, cols)
    q1 = jnp.dot(lhs, centre[1], preferred_element_type=F32).reshape(tiles, 2, tracks, cols)
    parts = (q0[:, 0] - q1[:, 1], q1[:, 0] + q0[:, 1])
    for k, part in enumerate(parts):
        part = part.reshape(many, cols).astype(BF16).astype(F32)
        at = slice(k * many, (k + 1) * many)
        for n in range(2):
            held = own_ref[n, at] + near_ref[n, at].astype(F32)
            out_ref[n, at] = held + part[:, n * half : (n + 1) * half]


def fold(steer_ref, out_ref):
    _, tracks, heights = steer_ref.shape
    same = lax.broadcasted_iota(jnp.int32, (heights, heights), 0)
    same = (same == lax.broadcasted_iota(jnp.int32, (heights, heights), 1)).astype(BF16)
    width = out_ref.shape[1]

    def turned(x):
        return lax.dot_general(same, x, (((1,), (1,)), ((), ())), preferred_element_type=F32).astype(BF16)

    def put(x, *starts):
        row = lax.broadcasted_iota(jnp.int32, (tracks, width), 0)
        col = lax.broadcasted_iota(jnp.int32, (tracks, width), 1)
        where = functools.reduce(jnp.logical_or, [col == row + start * tracks for start in starts])
        return jnp.dot(x, where.astype(BF16), preferred_element_type=F32)

    high, low = [], []
    for part in range(2):
        whole = steer_ref[part]
        top = whole.astype(BF16)
        high.append(turned(top))
        low.append(turned((whole - top.astype(F32)).astype(BF16)))
    real = put(high[0], 0, 2) + put(-high[1], 1, 3) + put(low[0], 4) + put(-low[1], 5)
    imag = put(high[1], 0, 2) + put(high[0], 1, 3) + put(low[1], 4) + put(low[0], 5)
    out_ref[:heights] = real.astype(BF16)
    out_ref[heights:] = imag.astype(BF16)


def focus(own_ref, mid_ref, next_ref, far_ref, matrix_ref, out_hbm, pieces, out, sem):
    _, lines, tiles, half = out.shape
    tracks = own_ref.shape[1] // (2 * tiles)
    odd = lax.rem(lax.axis_index("track"), 2)
    for k in range(2):
        total = own_ref[k] + mid_ref[k].astype(F32)
        total += next_ref[k].astype(F32)
        total += jnp.where(odd == k, far_ref[...].astype(F32), 0.0)
        high = total.astype(BF16)
        low = (total - high.astype(F32)).astype(BF16)
        cols = slice(k * half, (k + 1) * half)
        for part in range(2):
            for tile in range(tiles):
                start = (part * tiles + tile) * tracks
                for place, piece in enumerate((high, low, high)):
                    to = (2 * place + part) * tracks
                    pieces[tile, to : to + tracks, cols] = piece[start : start + tracks]

    steps = sem.shape[0]
    count = lines // steps
    copies = []
    for i in range(steps):
        matrix = matrix_ref[i * count : (i + 1) * count]
        for tile in range(tiles):
            sums = jnp.dot(matrix, pieces[tile], preferred_element_type=F32)
            for k in range(2):
                flat = out.at[k].reshape(lines * tiles, half)
                flat[pl.ds(i * count * tiles + tile, count, stride=tiles)] = sums[:, k * half : (k + 1) * half]
        here = pl.ds(i * count, count)
        for k in range(2):
            copy = pltpu.make_async_copy(
                out.at[k, here], out_hbm.at[here, :, k * half : (k + 1) * half], sem.at[i, k]
            )
            copy.start()
            copies.append(copy)
    for copy in copies:
        copy.wait()


def placed_in(x, name):
    return pltpu.with_memory_space_constraint(x, pltpu.MemorySpace[name])


def body(panels, kernel, steering, beam_strips, range_blocks):
    peers = lax.axis_size("track")
    blocks = beam_strips.shape[0]
    beams, _, span, footprint = kernel.shape
    tiles = range_blocks.shape[1]
    tracks = panels.shape[3]
    heights = steering.shape[1]
    half = footprint // 4
    rows = 2 * tiles * tracks

    def halves(count, dtype):
        return jax.ShapeDtypeStruct((count, rows, half), dtype)

    def send(x, to):
        return lax.ppermute(x, "track", [(i, to(i)) for i in range(peers) if 0 <= to(i) < peers])

    swap, cross, mid, far, near, own, nxt, picked, centre = pl.pallas_call(
        backproject,
        out_shape=(
            halves(2, BF16), halves(2, BF16), halves(2, BF16), jax.ShapeDtypeStruct((rows, half), BF16),
            halves(2, F32), halves(2, F32), halves(2, F32),
            jax.ShapeDtypeStruct((tiles, 2, tracks, span), BF16),
            jax.ShapeDtypeStruct((2, span, footprint // 2), BF16),
        ),
        in_specs=[HBM_SPEC] * 4,
        out_specs=(VMEM_SPEC,) * 9,
        scratch_shapes=[
            pltpu.SMEM((beams, blocks), jnp.int32),
            pltpu.SMEM((tiles, blocks), jnp.int32),
            pltpu.VMEM((beams, tiles, 2, tracks, span), BF16),
            pltpu.VMEM((beams, 2, span, footprint // 2), BF16),
            pltpu.VMEM((beams, 2, span, footprint // 2), BF16),
            pltpu.VMEM((14, rows, half), F32),
            pltpu.SemaphoreType.DMA((2,)),
            pltpu.SemaphoreType.DMA((beams + 1,)),
            pltpu.SemaphoreType.DMA((2 * beams + 1,)),
        ],
        compiler_params=pltpu.CompilerParams(vmem_limit_bytes=24 << 20),
        cost_estimate=pl.CostEstimate(
            flops=2 * 2 * beams * rows * span * footprint, bytes_accessed=16 << 20, transcendentals=0
        ),
    )(*(placed_in(x, "HBM") for x in (beam_strips.T, range_blocks.T, panels, kernel)))

    swapped = send(swap, lambda i: i ^ 1)
    crossed = send(cross, lambda i: i ^ 1)
    far_got = send(far, lambda i: i + 3 if i % 2 else i - 3)
    next_sum = (nxt + crossed.astype(F32)).astype(BF16)
    near_sum = (near + swapped.astype(F32)).astype(BF16)
    next_got = send(next_sum, lambda i: i + 2 if i // 2 % 2 else i - 2)
    near_got = send(near_sum, lambda i: i ^ 3)
    mid_got = send(mid, lambda i: i ^ 1)

    matrix = pl.pallas_call(
        fold,
        out_shape=jax.ShapeDtypeStruct((2 * heights, 6 * tracks), BF16),
        in_specs=[VMEM_SPEC],
        out_specs=VMEM_SPEC,
        compiler_params=pltpu.CompilerParams(vmem_limit_bytes=12 << 20),
        cost_estimate=pl.CostEstimate(flops=10_000_000, bytes_accessed=1 << 15, transcendentals=0),
    )(steering.transpose(0, 2, 1))

    own = pl.pallas_call(
        finish_own,
        out_shape=halves(2, F32),
        in_specs=[VMEM_SPEC] * 4,
        out_specs=VMEM_SPEC,
        compiler_params=pltpu.CompilerParams(vmem_limit_bytes=12 << 20),
        cost_estimate=pl.CostEstimate(flops=2 * rows * span * footprint, bytes_accessed=1 << 20, transcendentals=0),
    )(*(placed_in(x, "VMEM") for x in (picked, centre, own, near_got)))

    steps = 2
    volume = pl.pallas_call(
        focus,
        out_shape=jax.ShapeDtypeStruct((2 * heights, tiles, 2 * half), F32),
        in_specs=[VMEM_SPEC] * 5,
        out_specs=HBM_SPEC,
        scratch_shapes=[
            pltpu.VMEM((tiles, 6 * tracks, 2 * half), BF16),
            pltpu.VMEM((2, 2 * heights, tiles, half), F32),
            pltpu.SemaphoreType.DMA((steps, 2)),
        ],
        compiler_params=pltpu.CompilerParams(vmem_limit_bytes=12 << 20),
        cost_estimate=pl.CostEstimate(flops=100_000_000, bytes_accessed=2 << 20, transcendentals=0),
    )(*(placed_in(x, "VMEM") for x in (own, mid_got, next_got, far_got, matrix)))
    return volume.reshape(2, heights, tiles, 2 * half)


def solution(mesh):
    placed = (
        P(("scene", "track"), None, None, None, None),
        P(),
        P(),
        P("scene", None),
        P("scene", None),
    )
    return jax.shard_map(
        body, mesh=mesh, in_specs=placed, out_specs=P(None, None, "scene", "track"), check_vma=False
    )
```

```python
import functools

import jax
import jax.numpy as jnp
from jax import lax
from jax.experimental import pallas as pl
from jax.experimental.pallas import tpu as pltpu
from jax.sharding import PartitionSpec as P


F32 = jnp.float32
BF16 = jnp.bfloat16
VMEM_SPEC = pl.BlockSpec(memory_space=pltpu.VMEM)
HBM_SPEC = pl.BlockSpec(memory_space=pltpu.MemorySpace.HBM)


def backproject(
    strips_hbm, ranges_hbm, panel_hbm, kernel_hbm,
    swap_ref, cross_ref, mid_ref, far_ref, near_ref, own_ref, next_ref, own_rows, centre,
    strips_ref, ranges_ref, rows, edges, middles, slots, table_sem, row_sem, tap_sem,
):
    block = lax.axis_index("track")
    beams, _, span, footprint = kernel_hbm.shape
    tiles = ranges_ref.shape[0]
    tracks = panel_hbm.shape[3]
    half = footprint // 4
    cols = footprint // 2
    many = tiles * tracks
    inner = slice(half, half + cols)

    tables = [
        pltpu.make_async_copy(strips_hbm, strips_ref, table_sem.at[0]),
        pltpu.make_async_copy(ranges_hbm, ranges_ref, table_sem.at[1]),
    ]
    for copy in tables:
        copy.start()

    def fetch_edges(j):
        for k, q in enumerate((0, 3)):
            pltpu.make_async_copy(
                kernel_hbm.at[j, :, :, q * half : (q + 1) * half],
                edges.at[j, :, :, k * half : (k + 1) * half],
                tap_sem.at[j],
            ).start()

    order = [beams // 2] + [j for j in range(beams) if j != beams // 2]
    fetch_edges(order[0])
    for copy in tables:
        copy.wait()
    strip = [strips_ref[j, block] for j in range(beams)]
    shift = jnp.int32(0)
    for j in range(beams):
        shift = jnp.where(strip[j] >= 0, strip[j] + 1 - j - block, shift)
    base = 2 * shift + 3
    mine = 1 - shift
    for j in order:
        safe = jnp.maximum(strip[j], 0)
        for t in range(tiles):
            pltpu.make_async_copy(panel_hbm.at[0, ranges_ref[t, safe]], rows.at[j, t], row_sem.at[j]).start()
        if j != order[0]:
            fetch_edges(j)
    for j in order:

        @pl.when(j != mine)
        def _():
            pltpu.make_async_copy(kernel_hbm.at[j, :, :, inner], middles.at[j], tap_sem.at[beams + j]).start()

    for t in range(tiles):
        pltpu.make_async_copy(panel_hbm.at[0, ranges_ref[t, block]], own_rows.at[t], row_sem.at[beams]).start()
    last = pltpu.make_async_copy(kernel_hbm.at[mine, :, :, inner], centre, tap_sem.at[2 * beams])
    last.start()
    slots[...] = jnp.zeros_like(slots)

    def add(lhs, taps, targets):
        q0 = jnp.dot(lhs, taps[0], preferred_element_type=F32).reshape(tiles, 2, tracks, cols)
        q1 = jnp.dot(lhs, taps[1], preferred_element_type=F32).reshape(tiles, 2, tracks, cols)
        parts = (q0[:, 0] - q1[:, 1], q1[:, 0] + q0[:, 1])
        for k, part in enumerate(parts):
            part = part.reshape(many, cols).astype(BF16).astype(F32)
            for n, target in enumerate(targets):
                slots[target, k * many : (k + 1) * many] += part[:, n * half : (n + 1) * half]

    for j in order:
        pltpu.make_async_copy(panel_hbm.at[0, 0:tiles], rows.at[j], row_sem.at[j]).wait()
        pltpu.make_async_copy(kernel_hbm.at[j, :, :, inner], edges.at[j], tap_sem.at[j]).wait()

        @pl.when(strip[j] >= 0)
        def _():
            lhs = rows[j].reshape(2 * many, span)
            add(lhs, edges.at[j], (base + 2 * j, base + 2 * j + 3))

    for j in order:
        whole = pltpu.make_async_copy(kernel_hbm.at[j, :, :, inner], middles.at[j], tap_sem.at[beams + j])

        @pl.when(j != mine)
        def _():
            whole.wait()

        @pl.when((j != mine) & (strip[j] >= 0))
        def _():
            lhs = rows[j].reshape(2 * many, span)
            add(lhs, middles.at[j], (base + 2 * j + 1, base + 2 * j + 2))

    odd = lax.rem(block, 2)
    first = 4 * (1 - odd)
    upward = 8 * (1 - lax.rem(block // 2, 2))
    for k in range(2):
        swap_ref[k] = slots[2 + upward + k].astype(BF16)
        cross_ref[k] = slots[first + 8 - upward + k].astype(BF16)
        near_ref[k] = slots[first + upward + k]
        next_ref[k] = slots[10 - upward + k]
        mid_ref[k] = slots[first + 4 + k].astype(BF16)
        own_ref[k] = slots[6 + k]
    far_ref[...] = slots[jnp.where(odd == 1, 12, 1)].astype(BF16)
    pltpu.make_async_copy(panel_hbm.at[0, 0:tiles], own_rows, row_sem.at[beams]).wait()
    last.wait()


def finish_own(rows, centre, own_ref, near_ref, out_ref):
    tiles, _, tracks, span = rows.shape
    cols = centre.shape[2]
    half = cols // 2
    many = tiles * tracks
    lhs = rows[...].reshape(2 * many, span)
    q0 = jnp.dot(lhs, centre[0], preferred_element_type=F32).reshape(tiles, 2, tracks, cols)
    q1 = jnp.dot(lhs, centre[1], preferred_element_type=F32).reshape(tiles, 2, tracks, cols)
    parts = (q0[:, 0] - q1[:, 1], q1[:, 0] + q0[:, 1])
    for k, part in enumerate(parts):
        part = part.reshape(many, cols).astype(BF16).astype(F32)
        at = slice(k * many, (k + 1) * many)
        for n in range(2):
            held = own_ref[n, at] + near_ref[n, at].astype(F32)
            out_ref[n, at] = held + part[:, n * half : (n + 1) * half]


def fold(steer_ref, out_ref):
    _, tracks, heights = steer_ref.shape
    same = lax.broadcasted_iota(jnp.int32, (heights, heights), 0)
    same = (same == lax.broadcasted_iota(jnp.int32, (heights, heights), 1)).astype(BF16)
    width = out_ref.shape[1]

    def turned(x):
        return lax.dot_general(same, x, (((1,), (1,)), ((), ())), preferred_element_type=F32).astype(BF16)

    def put(x, *starts):
        row = lax.broadcasted_iota(jnp.int32, (tracks, width), 0)
        col = lax.broadcasted_iota(jnp.int32, (tracks, width), 1)
        where = functools.reduce(jnp.logical_or, [col == row + start * tracks for start in starts])
        return jnp.dot(x, where.astype(BF16), preferred_element_type=F32)

    high, low = [], []
    for part in range(2):
        whole = steer_ref[part]
        top = whole.astype(BF16)
        high.append(turned(top))
        low.append(turned((whole - top.astype(F32)).astype(BF16)))
    real = put(high[0], 0, 2) + put(-high[1], 1, 3) + put(low[0], 4) + put(-low[1], 5)
    imag = put(high[1], 0, 2) + put(high[0], 1, 3) + put(low[1], 4) + put(low[0], 5)
    out_ref[:heights] = real.astype(BF16)
    out_ref[heights:] = imag.astype(BF16)


def focus(own_ref, mid_ref, next_ref, far_ref, matrix_ref, out_hbm, pieces, out, sem):
    _, lines, tiles, half = out.shape
    tracks = own_ref.shape[1] // (2 * tiles)
    odd = lax.rem(lax.axis_index("track"), 2)
    copies = []
    for k in range(2):
        total = own_ref[k] + mid_ref[k].astype(F32)
        total += next_ref[k].astype(F32)
        total += jnp.where(odd == k, far_ref[...].astype(F32), 0.0)
        high = total.astype(BF16)
        low = (total - high.astype(F32)).astype(BF16)
        cols = slice(k * half, (k + 1) * half)
        for part in range(2):
            for tile in range(tiles):
                start = (part * tiles + tile) * tracks
                for place, piece in enumerate((high, low, high)):
                    to = (2 * place + part) * tracks
                    pieces[tile, to : to + tracks, cols] = piece[start : start + tracks]

        flat = out.at[k].reshape(lines * tiles, half)
        for tile in range(tiles):
            flat[pl.ds(tile, lines, stride=tiles)] = jnp.dot(
                matrix_ref[...], pieces[tile, :, cols], preferred_element_type=F32
            )
        copy = pltpu.make_async_copy(out.at[k], out_hbm.at[:, :, cols], sem.at[k])
        copy.start()
        copies.append(copy)
    for copy in copies:
        copy.wait()


def placed_in(x, name):
    return pltpu.with_memory_space_constraint(x, pltpu.MemorySpace[name])


def body(panels, kernel, steering, beam_strips, range_blocks):
    peers = lax.axis_size("track")
    blocks = beam_strips.shape[0]
    beams, _, span, footprint = kernel.shape
    tiles = range_blocks.shape[1]
    tracks = panels.shape[3]
    heights = steering.shape[1]
    half = footprint // 4
    rows = 2 * tiles * tracks

    def halves(count, dtype):
        return jax.ShapeDtypeStruct((count, rows, half), dtype)

    def send(x, to):
        return lax.ppermute(x, "track", [(i, to(i)) for i in range(peers) if 0 <= to(i) < peers])

    swap, cross, mid, far, near, own, nxt, picked, centre = pl.pallas_call(
        backproject,
        out_shape=(
            halves(2, BF16), halves(2, BF16), halves(2, BF16), jax.ShapeDtypeStruct((rows, half), BF16),
            halves(2, F32), halves(2, F32), halves(2, F32),
            jax.ShapeDtypeStruct((tiles, 2, tracks, span), BF16),
            jax.ShapeDtypeStruct((2, span, footprint // 2), BF16),
        ),
        in_specs=[HBM_SPEC] * 4,
        out_specs=(VMEM_SPEC,) * 9,
        scratch_shapes=[
            pltpu.SMEM((beams, blocks), jnp.int32),
            pltpu.SMEM((tiles, blocks), jnp.int32),
            pltpu.VMEM((beams, tiles, 2, tracks, span), BF16),
            pltpu.VMEM((beams, 2, span, footprint // 2), BF16),
            pltpu.VMEM((beams, 2, span, footprint // 2), BF16),
            pltpu.VMEM((14, rows, half), F32),
            pltpu.SemaphoreType.DMA((2,)),
            pltpu.SemaphoreType.DMA((beams + 1,)),
            pltpu.SemaphoreType.DMA((2 * beams + 1,)),
        ],
        compiler_params=pltpu.CompilerParams(vmem_limit_bytes=24 << 20),
        cost_estimate=pl.CostEstimate(
            flops=2 * 2 * beams * rows * span * footprint, bytes_accessed=16 << 20, transcendentals=0
        ),
    )(*(placed_in(x, "HBM") for x in (beam_strips.T, range_blocks.T, panels, kernel)))

    swapped = send(swap, lambda i: i ^ 1)
    crossed = send(cross, lambda i: i ^ 1)
    far_got = send(far, lambda i: i + 3 if i % 2 else i - 3)
    next_sum = (nxt + crossed.astype(F32)).astype(BF16)
    near_sum = (near + swapped.astype(F32)).astype(BF16)
    next_got = send(next_sum, lambda i: i + 2 if i // 2 % 2 else i - 2)
    near_got = send(near_sum, lambda i: i ^ 3)
    mid_got = send(mid, lambda i: i ^ 1)

    matrix = pl.pallas_call(
        fold,
        out_shape=jax.ShapeDtypeStruct((2 * heights, 6 * tracks), BF16),
        in_specs=[VMEM_SPEC],
        out_specs=VMEM_SPEC,
        compiler_params=pltpu.CompilerParams(vmem_limit_bytes=12 << 20),
        cost_estimate=pl.CostEstimate(flops=10_000_000, bytes_accessed=1 << 15, transcendentals=0),
    )(steering.transpose(0, 2, 1))

    own = pl.pallas_call(
        finish_own,
        out_shape=halves(2, F32),
        in_specs=[VMEM_SPEC] * 4,
        out_specs=VMEM_SPEC,
        compiler_params=pltpu.CompilerParams(vmem_limit_bytes=12 << 20),
        cost_estimate=pl.CostEstimate(flops=2 * rows * span * footprint, bytes_accessed=1 << 20, transcendentals=0),
    )(*(placed_in(x, "VMEM") for x in (picked, centre, own, near_got)))

    volume = pl.pallas_call(
        focus,
        out_shape=jax.ShapeDtypeStruct((2 * heights, tiles, 2 * half), F32),
        in_specs=[VMEM_SPEC] * 5,
        out_specs=HBM_SPEC,
        scratch_shapes=[
            pltpu.VMEM((tiles, 6 * tracks, 2 * half), BF16),
            pltpu.VMEM((2, 2 * heights, tiles, half), F32),
            pltpu.SemaphoreType.DMA((2,)),
        ],
        compiler_params=pltpu.CompilerParams(vmem_limit_bytes=12 << 20),
        cost_estimate=pl.CostEstimate(flops=100_000_000, bytes_accessed=2 << 20, transcendentals=0),
    )(*(placed_in(x, "VMEM") for x in (own, mid_got, next_got, far_got, matrix)))
    return volume.reshape(2, heights, tiles, 2 * half)


def solution(mesh):
    placed = (
        P(("scene", "track"), None, None, None, None),
        P(),
        P(),
        P("scene", None),
        P("scene", None),
    )
    return jax.shard_map(
        body, mesh=mesh, in_specs=placed, out_specs=P(None, None, "scene", "track"), check_vma=False
    )
```
